32 devices in a mesh: wide: 16 (over z, y, core), narrow: 2 (over x).
Axes of the slice: x: 2, y: 2, z: 4, core: 2. Of those that a mesh axis runs over, the one named last changes fastest.
Arguments:
- shocks: bfloat16 [64, 4096], replicated, may hold values from -6 to 6
- load_tiles: bfloat16 [32, 128, 128], P('narrow'), may hold values from -0.5 to 0.5
- load_index: int32 [32, 2], P('narrow'), may hold values from 0 to 31, as said below
- delta_tiles: bfloat16 [1024, 128, 128], P('wide'), may hold values from -0.09375 to 0.09375
- delta_index: int32 [256, 4], P('wide'), may hold values from 0 to 31, all different within a row
- base_value: float32 [32768], P('wide'), may hold values from -3 to 3
- trade_set: int32 [32768], P('wide'), may hold values from 0 to 2047, as said below
- set_slot: int32 [2048], replicated, may hold values from 0 to 2047, as said below
- default_step: int32 [64, 2048], P('narrow', 'wide'), may hold values from 0 to 7
Outputs:
- epe: float32 [2048], P('wide')
- default_loss: float32 [2048], P('wide')
The draws below stay inside these ranges and needn't reach their ends.
Inputs may be any that keep to these rules, and one draw needn't show every extreme that they name: load_index[i] = (row block, column block); the column blocks of the tiles of narrow index j lie in j * 16 to (j + 1) * 16 - 1, and no pair repeats. `delta_index`: the 4 factor blocks of one trade block differ. `set_slot`: A permutation of the netting sets. `trade_set`: of the 2048 trades of one index of wide, at most 256 have sets of one owner (set_slot // 128); one owner gets exactly 256 from every index of wide.
All inputs are finite; a program needn't handle non-finite values.
Results may differ from the reference program's by a relative error of at most 0.00046.
Values may be sent and summed in bfloat16 or wider, within the bound.
A program may use at most 64 MiB of HBM per device.

```python
import jax
import jax.numpy as jnp
from jax import lax

F = 4096
BLOCK = 128
LT_DEV = 16
DT_BLK = 4
NS_DEV = 128
STEPS = 8
STEP = 3
FB = 32
RB_DEV = 16
S = 64
L_TILES = 32
TR_DEV = 2048
TBLOCKS = 256
TRADES = 32768
NS = 2048
CAP = 256
N_WIDE = 16
N_NARROW = 2


def netting_layout(key):
    inverse = jax.random.permutation(jax.random.fold_in(key, 11), NS)
    favourite = jax.random.randint(jax.random.fold_in(key, 12), (), 0, N_WIDE)

    def one_device(device):
        device_key = jax.random.fold_in(key, 1000 + device)
        ranks = jax.random.permutation(jax.random.fold_in(device_key, 1), N_WIDE * CAP)
        owner_of = jnp.arange(N_WIDE * CAP, dtype=jnp.int32) // CAP
        score = jnp.where(owner_of == favourite, ranks - N_WIDE * CAP, ranks)
        chosen = jnp.argsort(score, stable=True)[:TR_DEV]
        shuffle = jax.random.permutation(jax.random.fold_in(device_key, 2), TR_DEV)
        owners = (chosen // CAP)[shuffle]
        local = jax.random.randint(jax.random.fold_in(device_key, 3), (TR_DEV,), 0, NS_DEV)
        return inverse[owners * NS_DEV + local]
    trades = jax.vmap(one_device)(jnp.arange(N_WIDE)).reshape(-1).astype(jnp.int32)
    slots = jnp.argsort(inverse, stable=True).astype(jnp.int32)
    return (trades, slots)


def draw_trade_set(key, part):
    return netting_layout(jax.random.fold_in(key, 5))[0]


def draw_set_slot(key, part):
    return netting_layout(jax.random.fold_in(key, 5))[1]


def draw_load_index(key, part):

    def one_group(group):
        picks = jax.random.permutation(jax.random.fold_in(key, 300 + group), RB_DEV * FB)[:LT_DEV]
        rows = picks // RB_DEV
        columns = group * RB_DEV + picks % RB_DEV
        return jnp.stack([rows, columns], axis=1)
    return jax.vmap(one_group)(jnp.arange(N_NARROW)).reshape(L_TILES, 2).astype(jnp.int32)


def place_ends(array, stream_key, least, top_value):
    place = [jax.random.randint(jax.random.fold_in(stream_key, axis), (), 0, length) for axis, length in enumerate(array.shape)]
    main_axis = array.shape.index(max(array.shape))
    neighbour = place[:main_axis] + [(place[main_axis] + 1) % array.shape[main_axis]] + place[main_axis + 1:]
    return array.at[tuple(place)].set(least).at[tuple(neighbour)].set(top_value)


def block_scale(own_key, extent, pieces, smallest, top_value):
    gain, own = 1.0, jax.random.fold_in(own_key, 6)
    for dim, blocks in pieces:
        steps = jnp.exp(jax.random.uniform(jax.random.fold_in(own, dim), (blocks,), jnp.float32, smallest / len(pieces), top_value / len(pieces)))
        gain = gain * jnp.repeat(steps, extent[dim] // blocks).reshape([-1 if axis == dim else 1 for axis in range(len(extent))])
    return gain


def picks_of(stream_key, rows, count, top, lift):
    sequence = jax.random.permutation(jax.random.fold_in(stream_key, 1), count)
    boost = sequence
    for power in range(3):
        boost = boost * boost // count
    boost = boost * lift // count
    tickets = jax.random.randint(jax.random.fold_in(stream_key, 2), (rows, count), 0, 4096) + boost
    sure = jax.random.permutation(jax.random.fold_in(stream_key, 3), rows)[jnp.arange(count) % rows]
    tickets = jnp.where(jnp.arange(rows)[:, None] == sure[None, :], 1 << 14, tickets)
    score = tickets * count + jnp.arange(count)
    return lax.top_k(score.astype(jnp.int32), top)[1].astype(jnp.int32)


def noise(key, extent, spread, bound, split=(), held_as=jnp.bfloat16):
    loudness = block_scale(key, extent, split, -0.22, 0.18) if split else 1.0
    drawn = jax.random.normal(key, extent, jnp.float32) * spread * loudness
    return jnp.minimum(jnp.maximum(drawn, -bound), bound).astype(held_as)


def setup_inputs(seed: int = 0) -> dict:
    keys = jax.random.split(jax.random.key(seed), 10)
    return {
        "shocks": noise(keys[0], (S, F), 1.0, 6.0),
        "load_tiles": noise(keys[1], (L_TILES, BLOCK, BLOCK), (BLOCK * LT_DEV // RB_DEV) ** -0.5, 0.5, ((0, 2),)),
        "load_index": draw_load_index(jax.random.fold_in(keys[9], 71), 0),
        "delta_tiles": noise(keys[3], (TBLOCKS * DT_BLK, BLOCK, BLOCK), (BLOCK * DT_BLK * 8) ** -0.5, 0.09375, ((0, 16),)),
        "delta_index": picks_of(keys[4], TBLOCKS, FB, DT_BLK, 1024),
        "base_value": noise(keys[5], (TRADES,), 0.5, 3.0, ((0, 16),), jnp.float32),
        "trade_set": draw_trade_set(jax.random.fold_in(keys[9], 71), 0),
        "set_slot": draw_set_slot(jax.random.fold_in(keys[9], 71), 0),
        "default_step": place_ends(jax.random.randint(keys[8], (S, NS), 0, STEPS), jax.random.fold_in(keys[8], 1), 0, STEPS - 1).astype(jnp.int32),
    }


def reference(shocks, load_tiles, load_index, delta_tiles, delta_index, base_value, trade_set, set_slot, default_step):
    shock_blocks = shocks.reshape(S, FB, BLOCK)
    start = shocks.astype(jnp.float32)

    def add_tile(index, total):
        row_block = load_index[index, 0].astype(jnp.int32)
        col_block = load_index[index, 1].astype(jnp.int32)
        picked = jnp.take(shock_blocks, row_block, axis=1)
        part = jnp.dot(picked, load_tiles[index], preferred_element_type=jnp.float32)
        offset = (col_block * BLOCK).astype(jnp.int32)
        column = lax.dynamic_slice_in_dim(total, offset, BLOCK, 1)
        return lax.dynamic_update_slice_in_dim(total, column + part, offset, 1)

    moves = lax.fori_loop(0, L_TILES, add_tile, start).astype(jnp.bfloat16)
    move_blocks = moves.reshape(S, FB, BLOCK)
    tile_groups = delta_tiles.reshape(TBLOCKS, DT_BLK, BLOCK, BLOCK)

    def value_block(inputs):
        tiles, factor_blocks = inputs
        picked = jnp.take(move_blocks, factor_blocks, axis=1)
        return jnp.einsum('ska,kat->st', picked.astype(jnp.float32), tiles.astype(jnp.float32))

    valued = lax.map(value_block, (tile_groups, delta_index))
    values = jnp.transpose(valued, (0, 2, 1)).reshape(TRADES, S) + base_value[:, None]
    slots = jnp.take(set_slot, trade_set)
    netted = jax.ops.segment_sum(values, slots, num_segments=NS)
    exposure = jnp.maximum(netted, 0.0)
    hit = (default_step.T == STEP).astype(jnp.float32)
    epe = jnp.sum(exposure, axis=1) / S
    default_loss = jnp.sum(hit * exposure, axis=1) * (STEPS / S)
    return epe, default_loss
```

```python
import functools

import jax
import jax.numpy as jnp
from jax import lax
from jax.experimental import pallas as pl
from jax.experimental.pallas import tpu as pltpu
from jax.sharding import PartitionSpec as P

BLOCK = 128
STEPS = 8
STEP = 3
MESH = pl.DeviceIdType.MESH
F32 = jnp.float32
BF16 = jnp.bfloat16


def one_hot(row, size):
    lane = lax.broadcasted_iota(jnp.int32, (size, row.shape[1]), 0)
    return jnp.where(lane == row, 1.0, 0.0)


def kernel(
    narrow_count,
    wide_count,
    shocks,
    load_tiles,
    load_index,
    delta_tiles,
    delta_index,
    base,
    trade_set,
    set_slot,
    default_step,
    epe,
    default_loss,
    shock_blocks,
    moves_out,
    moves,
    parts,
    deltas,
    member,
    pair_mask,
    high,
    low,
    partial,
    got_pair,
    halved,
    got_wide,
    sums,
    delta_sem,
    move_send,
    move_recv,
    pair_send,
    pair_recv,
    wide_send,
    wide_recv,
    sum_send,
    sum_recv,
):
    group = lax.axis_index("narrow")
    wide = lax.axis_index("wide")
    couples = wide_count // 2
    couple = wide // 2
    parity = lax.rem(wide, 2)
    scen_all = shocks.shape[0]
    own_blocks = moves_out.shape[1]
    scen_dev = moves.shape[1]
    tiles = load_tiles.shape[0]
    trade_blocks, per_block = delta_index.shape
    own_sets = default_step.shape[1]
    span = 2 * own_sets
    bits = span.bit_length() - 1

    fetch = pltpu.make_async_copy(delta_tiles, deltas, delta_sem)
    fetch.start()
    narrow_peers = [lax.rem(group + k, narrow_count) for k in range(1, narrow_count)]
    wide_peers = [lax.rem(couple + k, couples) * 2 + parity for k in range(1, couples)]
    partner = couple * 2 + 1 - parity
    barrier = pltpu.get_barrier_semaphore()
    for peer in narrow_peers:
        pl.semaphore_signal(barrier, inc=1, device_id={"narrow": peer}, device_id_type=MESH)
    for peer in wide_peers + [partner]:
        pl.semaphore_signal(barrier, inc=1, device_id={"wide": peer}, device_id_type=MESH)

    for c in range(shock_blocks.shape[0]):
        shock_blocks[c] = shocks[:, c * BLOCK : (c + 1) * BLOCK]
    for i in range(tiles):
        parts[i] = jnp.dot(
            shock_blocks[load_index[i, 0]], load_tiles[i], preferred_element_type=F32
        )
    columns = [jnp.full((1, BLOCK), load_index[i, 1]) for i in range(tiles)]
    for c in range(own_blocks):
        column = group * own_blocks + c
        total = shock_blocks[column].astype(F32)
        for i in range(tiles):
            total += parts[i] * jnp.where(columns[i] == column, 1.0, 0.0)
        rounded = total.astype(BF16)
        for n in range(narrow_count):
            moves_out[n, c] = rounded[n * scen_dev : (n + 1) * scen_dev]

    pl.semaphore_wait(barrier, len(narrow_peers) + len(wide_peers) + 1)
    own_rows = pl.ds(group * own_blocks, own_blocks)
    move_copies = [
        pltpu.make_async_remote_copy(
            src_ref=moves_out.at[peer],
            dst_ref=moves.at[own_rows],
            send_sem=move_send.at[k],
            recv_sem=move_recv.at[k],
            device_id={"narrow": peer},
            device_id_type=MESH,
        )
        for k, peer in enumerate(narrow_peers)
    ]
    for copy in move_copies:
        copy.start()
    moves[own_rows] = moves_out[group]

    slots = set_slot[...]
    digits = jnp.concatenate(
        [lax.shift_right_logical(slots, bits), lax.bitwise_and(slots, span - 1)], axis=0
    )
    table = digits.astype(F32).astype(BF16)
    set_rows = slots.shape[0]
    for b in range(trade_blocks):
        ids = trade_set[b : b + 1, :]
        low_hot = one_hot(lax.bitwise_and(ids, BLOCK - 1), BLOCK).astype(BF16)
        looked = jnp.dot(table, low_hot, preferred_element_type=F32)
        row_hot = one_hot(lax.shift_right_logical(ids, 7), set_rows)
        upper = jnp.sum(looked[:set_rows] * row_hot, axis=0, keepdims=True)
        lower = jnp.sum(looked[set_rows:] * row_hot, axis=0, keepdims=True)
        lanes = slice(b * BLOCK, (b + 1) * BLOCK)
        member[:, lanes] = one_hot(lower.astype(jnp.int32), span).astype(BF16)
        spread = jnp.broadcast_to(upper, (scen_dev, BLOCK))
        for e in range(couples):
            pair_mask[e * scen_dev : (e + 1) * scen_dev, lanes] = jnp.where(
                spread == float(e), 1.0, 0.0
            ).astype(BF16)

    for copy in move_copies:
        copy.wait()
    fetch.wait()

    for b in range(trade_blocks):
        picked = jnp.concatenate(
            [moves[delta_index[b, k]] for k in range(per_block)], axis=1
        )
        block = deltas[b * per_block : (b + 1) * per_block].reshape(per_block * BLOCK, BLOCK)
        value = jnp.dot(picked, block, preferred_element_type=F32) + base[b : b + 1, :]
        first = value.astype(BF16)
        second = (value - first.astype(F32)).astype(BF16)
        lanes = slice(b * BLOCK, (b + 1) * BLOCK)
        for e in range(couples):
            rows = slice(e * scen_dev, (e + 1) * scen_dev)
            mask = pair_mask[rows, lanes]
            high[rows, lanes] = first * mask
            low[rows, lanes] = second * mask
    contract = (((1,), (1,)), ((), ()))
    hot = member[...]
    netted = lax.dot_general(
        high[...], hot, contract, preferred_element_type=F32
    ) + lax.dot_general(low[...], hot, contract, preferred_element_type=F32)
    for e in range(couples):
        rows = slice(e * scen_dev, (e + 1) * scen_dev)
        partial[0, e] = netted[rows, :own_sets]
        partial[1, e] = netted[rows, own_sets:]

    swap = pltpu.make_async_remote_copy(
        src_ref=partial.at[1 - parity],
        dst_ref=got_pair,
        send_sem=pair_send,
        recv_sem=pair_recv,
        device_id={"wide": partner},
        device_id_type=MESH,
    )
    swap.start()
    swap.wait()
    halved[...] = partial[parity] + got_pair[...]
    wide_copies = [
        pltpu.make_async_remote_copy(
            src_ref=halved.at[lax.rem(couple + k + 1, couples)],
            dst_ref=got_wide.at[k],
            send_sem=wide_send.at[k],
            recv_sem=wide_recv.at[k],
            device_id={"wide": peer},
            device_id_type=MESH,
        )
        for k, peer in enumerate(wide_peers)
    ]
    for copy in wide_copies:
        copy.start()
    for copy in wide_copies:
        copy.wait()
    total = halved[couple]
    for k in range(len(wide_peers)):
        total += got_wide[k]

    exposure = jnp.maximum(total, 0.0)
    hit = jnp.where(default_step[...] == STEP, exposure, 0.0)
    sums[group, 0:1] = jnp.sum(exposure, axis=0, keepdims=True)
    sums[group, 1:2] = jnp.sum(hit, axis=0, keepdims=True)
    sum_copies = [
        pltpu.make_async_remote_copy(
            src_ref=sums.at[group],
            dst_ref=sums.at[group],
            send_sem=sum_send.at[k],
            recv_sem=sum_recv.at[k],
            device_id={"narrow": peer},
            device_id_type=MESH,
        )
        for k, peer in enumerate(narrow_peers)
    ]
    for copy in sum_copies:
        copy.start()
    for copy in sum_copies:
        copy.wait()
    both = sums[0]
    for n in range(1, narrow_count):
        both += sums[n]
    epe[...] = both[0:1] * (1.0 / scen_all)
    default_loss[...] = both[1:2] * (STEPS / scen_all)


def on_device(
    shocks,
    load_tiles,
    load_index,
    delta_tiles,
    delta_index,
    base_value,
    trade_set,
    set_slot,
    default_step,
):
    narrow_count = lax.axis_size("narrow")
    wide_count = lax.axis_size("wide")
    scen_all, width = shocks.shape
    factor_blocks = width // BLOCK
    own_blocks = factor_blocks // narrow_count
    scen_dev, own_sets = default_step.shape
    trades = trade_set.shape[0]
    couples = wide_count // 2
    lines = couples * scen_dev
    vmem = pl.BlockSpec(memory_space=pltpu.VMEM)
    smem = pl.BlockSpec(memory_space=pltpu.SMEM)
    dma = pltpu.SemaphoreType.DMA
    epe, default_loss = pl.pallas_call(
        functools.partial(kernel, narrow_count, wide_count),
        out_shape=(jax.ShapeDtypeStruct((1, own_sets), F32),) * 2,
        in_specs=[
            vmem,
            vmem,
            smem,
            pl.BlockSpec(memory_space=pl.ANY),
            smem,
            vmem,
            vmem,
            vmem,
            vmem,
        ],
        out_specs=(vmem, vmem),
        scratch_shapes=[
            pltpu.VMEM((factor_blocks, scen_all, BLOCK), BF16),
            pltpu.VMEM((narrow_count, own_blocks, scen_dev, BLOCK), BF16),
            pltpu.VMEM((factor_blocks, scen_dev, BLOCK), BF16),
            pltpu.VMEM((load_tiles.shape[0], scen_all, BLOCK), F32),
            pltpu.VMEM(delta_tiles.shape, BF16),
            pltpu.VMEM((2 * own_sets, trades), BF16),
            pltpu.VMEM((lines, trades), BF16),
            pltpu.VMEM((lines, trades), BF16),
            pltpu.VMEM((lines, trades), BF16),
            pltpu.VMEM((2, couples, scen_dev, own_sets), F32),
            pltpu.VMEM((couples, scen_dev, own_sets), F32),
            pltpu.VMEM((couples, scen_dev, own_sets), F32),
            pltpu.VMEM((couples - 1, scen_dev, own_sets), F32),
            pltpu.VMEM((narrow_count, 2, own_sets), F32),
            dma,
            dma((narrow_count - 1,)),
            dma((narrow_count - 1,)),
            dma,
            dma,
            dma((couples - 1,)),
            dma((couples - 1,)),
            dma((narrow_count - 1,)),
            dma((narrow_count - 1,)),
        ],
        compiler_params=pltpu.CompilerParams(collective_id=0, has_side_effects=True),
    )(
        shocks,
        load_tiles,
        load_index,
        delta_tiles,
        delta_index,
        base_value.reshape(-1, BLOCK),
        trade_set.reshape(-1, BLOCK),
        set_slot.reshape(-1, BLOCK),
        default_step,
    )
    return epe.reshape(-1), default_loss.reshape(-1)


def solution(mesh):
    return jax.shard_map(
        on_device,
        mesh=mesh,
        in_specs=(
            P(),
            P("narrow", None, None),
            P("narrow", None),
            P("wide", None, None),
            P("wide", None),
            P("wide"),
            P("wide"),
            P(),
            P("narrow", "wide"),
        ),
        out_specs=(P("wide"), P("wide")),
        check_vma=False,
    )
```

```python
import functools

import jax
import jax.numpy as jnp
from jax import lax
from jax.experimental import pallas as pl
from jax.experimental.pallas import tpu as pltpu
from jax.sharding import PartitionSpec as P

BLOCK = 128
STEPS = 8
STEP = 3
MESH = pl.DeviceIdType.MESH
F32 = jnp.float32
BF16 = jnp.bfloat16


def one_hot(row, size):
    lane = lax.broadcasted_iota(jnp.int32, (size, row.shape[1]), 0)
    return jnp.where(lane == row, 1.0, 0.0)


def kernel(
    narrow_count,
    wide_count,
    shocks_hbm,
    load_tiles_hbm,
    load_index_hbm,
    delta_tiles_hbm,
    delta_index_hbm,
    base_hbm,
    trade_set_hbm,
    set_slot_hbm,
    default_step_hbm,
    sums_out,
    shocks,
    load_tiles,
    load_index,
    delta_tiles,
    delta_index,
    base,
    trade_set,
    set_slot,
    default_step,
    shock_blocks,
    moves_out,
    moves,
    parts,
    member,
    pair_mask,
    spread_values,
    partial,
    got_pair,
    halved,
    got_wide,
    sums,
    fetch_sem,
    move_send,
    move_recv,
    pair_send,
    pair_recv,
    wide_send,
    wide_recv,
    sum_send,
    sum_recv,
):
    group = lax.axis_index("narrow")
    wide = lax.axis_index("wide")
    couples = wide_count // 2
    couple = wide // 2
    parity = lax.rem(wide, 2)
    own_blocks = moves_out.shape[1]
    scen_dev = moves.shape[1]
    tiles = load_tiles.shape[0]
    per_block, trade_blocks = delta_index.shape
    own_sets = default_step.shape[1]
    span = 2 * own_sets
    bits = span.bit_length() - 1
    half = couples // 2
    near = couple // half
    place = lax.rem(couple, half)

    narrow_peers = [lax.rem(group + k, narrow_count) for k in range(1, narrow_count)]
    targets = [(0, (1 - near) * half, lax.rem(place + k, half)) for k in range(half)]
    targets += [(1, near * half, lax.rem(place + k, half)) for k in range(1, half)]
    partner = couple * 2 + 1 - parity
    barrier = pltpu.get_barrier_semaphore()
    for _, start, j in targets:
        peer = (start + j) * 2 + parity
        pl.semaphore_signal(barrier, inc=1, device_id={"wide": peer}, device_id_type=MESH)
    for peer in narrow_peers:
        pl.semaphore_signal(barrier, inc=1, device_id={"narrow": peer}, device_id_type=MESH)
    pl.semaphore_signal(barrier, inc=1, device_id={"wide": partner}, device_id_type=MESH)
    fetches = [
        pltpu.make_async_copy(source, target, fetch_sem.at[i])
        for i, (source, target) in enumerate(
            (
                (shocks_hbm, shocks),
                (load_index_hbm, load_index),
                (load_tiles_hbm, load_tiles),
                (trade_set_hbm, trade_set),
                (set_slot_hbm, set_slot),
                (delta_index_hbm, delta_index),
                (delta_tiles_hbm, delta_tiles),
                (base_hbm, base),
                (default_step_hbm, default_step),
            )
        )
    ]
    for fetch in fetches:
        fetch.start()
    for fetch in fetches[:3]:
        fetch.wait()

    for c in range(shock_blocks.shape[0]):
        shock_blocks[c] = shocks[:, c * BLOCK : (c + 1) * BLOCK]
    for i in range(tiles):
        parts[i] = jnp.dot(
            shock_blocks[load_index[0, i]], load_tiles[i], preferred_element_type=F32
        )
    columns = [jnp.full((1, BLOCK), load_index[1, i]) for i in range(tiles)]
    for c in range(own_blocks):
        column = group * own_blocks + c
        total = shock_blocks[column].astype(F32)
        for i in range(tiles):
            total += parts[i] * jnp.where(columns[i] == column, 1.0, 0.0)
        rounded = total.astype(BF16)
        for n in range(narrow_count):
            moves_out[n, c] = rounded[n * scen_dev : (n + 1) * scen_dev]

    pl.semaphore_wait(barrier, len(narrow_peers) + len(targets) + 1)
    own_rows = pl.ds(group * own_blocks, own_blocks)
    move_copies = [
        pltpu.make_async_remote_copy(
            src_ref=moves_out.at[peer],
            dst_ref=moves.at[own_rows],
            send_sem=move_send.at[k],
            recv_sem=move_recv.at[k],
            device_id={"narrow": peer},
            device_id_type=MESH,
        )
        for k, peer in enumerate(narrow_peers)
    ]
    for copy in move_copies:
        copy.start()
    moves[own_rows] = moves_out[group]

    for fetch in fetches[3:]:
        fetch.wait()
    slots = set_slot[...]
    digits = jnp.concatenate(
        [lax.shift_right_logical(slots, bits), lax.bitwise_and(slots, span - 1)], axis=0
    )
    table = digits.astype(F32).astype(BF16)
    set_rows = slots.shape[0]
    for b in range(trade_blocks):
        ids = trade_set[b : b + 1, :]
        low_hot = one_hot(lax.bitwise_and(ids, BLOCK - 1), BLOCK).astype(BF16)
        looked = jnp.dot(table, low_hot, preferred_element_type=F32)
        row_hot = one_hot(lax.shift_right_logical(ids, 7), set_rows)
        upper = jnp.sum(looked[:set_rows] * row_hot, axis=0, keepdims=True)
        lower = jnp.sum(looked[set_rows:] * row_hot, axis=0, keepdims=True)
        lanes = slice(b * BLOCK, (b + 1) * BLOCK)
        member[:, lanes] = one_hot(lower.astype(jnp.int32), span).astype(BF16)
        spread = jnp.broadcast_to(upper, (scen_dev, BLOCK))
        for e in range(couples):
            pair_mask[e * scen_dev : (e + 1) * scen_dev, lanes] = jnp.where(
                spread == float(e), 1.0, 0.0
            ).astype(BF16)

    for copy in move_copies:
        copy.wait()

    for b in range(trade_blocks):
        picked = jnp.concatenate(
            [moves[delta_index[k, b]] for k in range(per_block)], axis=1
        )
        block = delta_tiles[b * per_block : (b + 1) * per_block].reshape(
            per_block * BLOCK, BLOCK
        )
        value = jnp.dot(picked, block, preferred_element_type=F32) + base[b : b + 1, :]
        first = value.astype(BF16)
        second = (value - first.astype(F32)).astype(BF16)
        lanes = slice(b * BLOCK, (b + 1) * BLOCK)
        for e in range(couples):
            mask = pair_mask[e * scen_dev : (e + 1) * scen_dev, lanes]
            row = (e % half) * scen_dev
            spread_values[e // half, row : row + scen_dev, lanes] = first * mask
            row += half * scen_dev
            spread_values[e // half, row : row + scen_dev, lanes] = second * mask
    swaps = []
    for step in range(2):
        netted = lax.dot_general(
            spread_values[1 - near if step == 0 else near],
            member[...],
            (((1,), (1,)), ((), ())),
            preferred_element_type=F32,
        )
        netted = netted[: half * scen_dev] + netted[half * scen_dev :]
        for j in range(half):
            rows = slice(j * scen_dev, (j + 1) * scen_dev)
            partial[0, step, j] = netted[rows, :own_sets]
            partial[1, step, j] = netted[rows, own_sets:]
        swap = pltpu.make_async_remote_copy(
            src_ref=partial.at[1 - parity, step],
            dst_ref=got_pair.at[step],
            send_sem=pair_send.at[step],
            recv_sem=pair_recv.at[step],
            device_id={"wide": partner},
            device_id_type=MESH,
        )
        swap.start()
        swaps.append(swap)

    wide_copies = []
    for step in range(2):
        swaps[step].wait()
        halved[step] = partial[parity, step] + got_pair[step]
        for k, (when, start, j) in enumerate(targets):
            if when == step:
                copy = pltpu.make_async_remote_copy(
                    src_ref=halved.at[step, j],
                    dst_ref=got_wide.at[k],
                    send_sem=wide_send.at[k],
                    recv_sem=wide_recv.at[k],
                    device_id={"wide": (start + j) * 2 + parity},
                    device_id_type=MESH,
                )
                copy.start()
                wide_copies.append(copy)
    total = halved[1, place]
    for k in range(len(targets) - 1, -1, -1):
        wide_copies[k].wait()
        total += got_wide[k]

    exposure = jnp.maximum(total, 0.0)
    hit = jnp.where(default_step[...] == STEP, exposure, 0.0)
    sums[group, 0:1] = jnp.sum(exposure, axis=0, keepdims=True)
    sums[group, 1:2] = jnp.sum(hit, axis=0, keepdims=True)
    sum_copies = [
        pltpu.make_async_remote_copy(
            src_ref=sums.at[group],
            dst_ref=sums.at[group],
            send_sem=sum_send.at[k],
            recv_sem=sum_recv.at[k],
            device_id={"narrow": peer},
            device_id_type=MESH,
        )
        for k, peer in enumerate(narrow_peers)
    ]
    for copy in sum_copies:
        copy.start()
    for copy in sum_copies:
        copy.wait()
    both = sums[0]
    for n in range(1, narrow_count):
        both += sums[n]
    sums_out[...] = both


def on_device(
    shocks,
    load_tiles,
    load_index,
    delta_tiles,
    delta_index,
    base_value,
    trade_set,
    set_slot,
    default_step,
):
    narrow_count = lax.axis_size("narrow")
    wide_count = lax.axis_size("wide")
    scen_all, width = shocks.shape
    factor_blocks = width // BLOCK
    own_blocks = factor_blocks // narrow_count
    scen_dev, own_sets = default_step.shape
    trades = trade_set.shape[0]
    couples = wide_count // 2
    lines = couples * scen_dev
    dma = pltpu.SemaphoreType.DMA
    arrays = (
        shocks,
        load_tiles,
        load_index.T,
        delta_tiles,
        delta_index.T,
        base_value.reshape(-1, BLOCK),
        trade_set.reshape(-1, BLOCK),
        set_slot.reshape(-1, BLOCK),
        default_step,
    )
    spaces = [pltpu.VMEM, pltpu.VMEM, pltpu.SMEM, pltpu.VMEM, pltpu.SMEM] + [pltpu.VMEM] * 4
    totals = pl.pallas_call(
        functools.partial(kernel, narrow_count, wide_count),
        out_shape=jax.ShapeDtypeStruct((2, own_sets), F32),
        in_specs=[pl.BlockSpec(memory_space=pl.ANY)] * len(arrays),
        out_specs=pl.BlockSpec(memory_space=pltpu.VMEM),
        scratch_shapes=[space(array.shape, array.dtype) for space, array in zip(spaces, arrays)]
        + [
            pltpu.VMEM((factor_blocks, scen_all, BLOCK), BF16),
            pltpu.VMEM((narrow_count, own_blocks, scen_dev, BLOCK), BF16),
            pltpu.VMEM((factor_blocks, scen_dev, BLOCK), BF16),
            pltpu.VMEM((load_tiles.shape[0], scen_all, BLOCK), F32),
            pltpu.VMEM((2 * own_sets, trades), BF16),
            pltpu.VMEM((lines, trades), BF16),
            pltpu.VMEM((2, lines, trades), BF16),
            pltpu.VMEM((2, 2, couples // 2, scen_dev, own_sets), F32),
            pltpu.VMEM((2, couples // 2, scen_dev, own_sets), F32),
            pltpu.VMEM((2, couples // 2, scen_dev, own_sets), F32),
            pltpu.VMEM((couples - 1, scen_dev, own_sets), F32),
            pltpu.VMEM((narrow_count, 2, own_sets), F32),
            dma((len(arrays),)),
            dma((narrow_count - 1,)),
            dma((narrow_count - 1,)),
            dma((2,)),
            dma((2,)),
            dma((couples - 1,)),
            dma((couples - 1,)),
            dma((narrow_count - 1,)),
            dma((narrow_count - 1,)),
        ],
        compiler_params=pltpu.CompilerParams(collective_id=0, has_side_effects=True),
    )(*arrays)
    return totals[0] / scen_all, totals[1] * (STEPS / scen_all)


def solution(mesh):
    return jax.shard_map(
        on_device,
        mesh=mesh,
        in_specs=(
            P(),
            P("narrow", None, None),
            P("narrow", None),
            P("wide", None, None),
            P("wide", None),
            P("wide"),
            P("wide"),
            P(),
            P("narrow", "wide"),
        ),
        out_specs=(P("wide"), P("wide")),
        check_vma=False,
    )
```

```python
import functools

import jax
import jax.numpy as jnp
from jax import lax
from jax.experimental import pallas as pl
from jax.experimental.pallas import tpu as pltpu
from jax.sharding import PartitionSpec as P

BLOCK = 128
STEPS = 8
STEP = 3
MESH = pl.DeviceIdType.MESH
F32 = jnp.float32
BF16 = jnp.bfloat16


def one_hot(row, size):
    lane = lax.broadcasted_iota(jnp.int32, (size, row.shape[1]), 0)
    return jnp.where(lane == row, 1.0, 0.0)


def kernel(
    narrow_count,
    wide_count,
    shocks_hbm,
    load_tiles_hbm,
    load_index_hbm,
    delta_tiles_hbm,
    delta_index_hbm,
    base_hbm,
    trade_set_hbm,
    set_slot_hbm,
    default_step_hbm,
    sums_out,
    shocks,
    load_tiles,
    load_index,
    delta_tiles,
    delta_index,
    base,
    trade_set,
    set_slot,
    default_step,
    shock_blocks,
    moves_out,
    moves,
    parts,
    member,
    pair_mask,
    spread_values,
    partial,
    got_pair,
    halved,
    got_wide,
    sums,
    fetch_sem,
    move_send,
    move_recv,
    pair_send,
    pair_recv,
    wide_send,
    wide_recv,
    sum_send,
    sum_recv,
):
    group = lax.axis_index("narrow")
    wide = lax.axis_index("wide")
    couples = wide_count // 2
    couple = wide // 2
    parity = lax.rem(wide, 2)
    own_blocks = moves_out.shape[1]
    scen_dev = moves.shape[1]
    tiles = load_tiles.shape[0]
    per_block, trade_blocks = delta_index.shape
    own_sets = default_step.shape[1]
    span = 2 * own_sets
    bits = span.bit_length() - 1
    half = couples // 2
    near = couple // half
    place = lax.rem(couple, half)

    narrow_peers = [lax.rem(group + k, narrow_count) for k in range(1, narrow_count)]
    targets = [(0, (1 - near) * half, lax.rem(place + k, half)) for k in range(half)]
    targets += [(1, near * half, lax.rem(place + k, half)) for k in range(1, half)]
    partner = couple * 2 + 1 - parity
    barrier = pltpu.get_barrier_semaphore()
    for _, start, j in targets:
        peer = (start + j) * 2 + parity
        pl.semaphore_signal(barrier, inc=1, device_id={"wide": peer}, device_id_type=MESH)
    for peer in narrow_peers:
        pl.semaphore_signal(barrier, inc=1, device_id={"narrow": peer}, device_id_type=MESH)
    pl.semaphore_signal(barrier, inc=1, device_id={"wide": partner}, device_id_type=MESH)
    fetches = [
        pltpu.make_async_copy(source, target, fetch_sem.at[i])
        for i, (source, target) in enumerate(
            (
                (shocks_hbm, shocks),
                (load_index_hbm, load_index),
                (load_tiles_hbm, load_tiles),
                (trade_set_hbm, trade_set),
                (set_slot_hbm, set_slot),
                (delta_index_hbm, delta_index),
                (delta_tiles_hbm, delta_tiles),
                (base_hbm, base),
                (default_step_hbm, default_step),
            )
        )
    ]
    for fetch in fetches:
        fetch.start()
    for fetch in fetches[:3]:
        fetch.wait()

    for c in range(shock_blocks.shape[0]):
        shock_blocks[c] = shocks[:, c * BLOCK : (c + 1) * BLOCK]
    for i in range(tiles):
        parts[i] = jnp.dot(
            shock_blocks[load_index[0, i]], load_tiles[i], preferred_element_type=F32
        )
    columns = [jnp.full((1, BLOCK), load_index[1, i]) for i in range(tiles)]
    for c in range(own_blocks):
        column = group * own_blocks + c
        total = shock_blocks[column].astype(F32)
        for i in range(tiles):
            total += parts[i] * jnp.where(columns[i] == column, 1.0, 0.0)
        rounded = total.astype(BF16)
        for n in range(narrow_count):
            moves_out[n, c] = rounded[n * scen_dev : (n + 1) * scen_dev]

    pl.semaphore_wait(barrier, len(narrow_peers) + len(targets) + 1)
    own_rows = pl.ds(group * own_blocks, own_blocks)
    move_copies = [
        pltpu.make_async_remote_copy(
            src_ref=moves_out.at[peer],
            dst_ref=moves.at[own_rows],
            send_sem=move_send.at[k],
            recv_sem=move_recv.at[k],
            device_id={"narrow": peer},
            device_id_type=MESH,
        )
        for k, peer in enumerate(narrow_peers)
    ]
    for copy in move_copies:
        copy.start()
    moves[own_rows] = moves_out[group]

    for fetch in fetches[3:]:
        fetch.wait()
    slots = set_slot[...]
    digits = jnp.concatenate(
        [lax.shift_right_logical(slots, bits), lax.bitwise_and(slots, span - 1)], axis=0
    )
    table = digits.astype(F32).astype(BF16)
    set_rows = slots.shape[0]
    for b in range(trade_blocks):
        ids = trade_set[b : b + 1, :]
        low_hot = one_hot(lax.bitwise_and(ids, BLOCK - 1), BLOCK).astype(BF16)
        looked = jnp.dot(table, low_hot, preferred_element_type=F32)
        row_hot = one_hot(lax.shift_right_logical(ids, 7), set_rows)
        upper = jnp.sum(looked[:set_rows] * row_hot, axis=0, keepdims=True)
        lower = jnp.sum(looked[set_rows:] * row_hot, axis=0, keepdims=True)
        lanes = slice(b * BLOCK, (b + 1) * BLOCK)
        member[:, lanes] = one_hot(lower.astype(jnp.int32), span).astype(BF16)
        spread = jnp.broadcast_to(upper, (scen_dev, BLOCK))
        for e in range(couples):
            pair_mask[e * scen_dev : (e + 1) * scen_dev, lanes] = jnp.where(
                spread == float(e), 1.0, 0.0
            ).astype(BF16)

    for copy in move_copies:
        copy.wait()

    for b in range(trade_blocks):
        picked = jnp.concatenate(
            [moves[delta_index[k, b]] for k in range(per_block)], axis=1
        )
        block = delta_tiles[b * per_block : (b + 1) * per_block].reshape(
            per_block * BLOCK, BLOCK
        )
        value = jnp.dot(picked, block, preferred_element_type=F32) + base[b : b + 1, :]
        first = value.astype(BF16)
        second = (value - first.astype(F32)).astype(BF16)
        lanes = slice(b * BLOCK, (b + 1) * BLOCK)
        for e in range(couples):
            mask = pair_mask[e * scen_dev : (e + 1) * scen_dev, lanes]
            row = (e % half) * scen_dev
            spread_values[e // half, row : row + scen_dev, lanes] = first * mask
            row += half * scen_dev
            spread_values[e // half, row : row + scen_dev, lanes] = second * mask
    swaps = []
    for step in range(2):
        netted = lax.dot_general(
            spread_values[1 - near if step == 0 else near],
            member[...],
            (((1,), (1,)), ((), ())),
            preferred_element_type=F32,
        )
        netted = netted[: half * scen_dev] + netted[half * scen_dev :]
        for j in range(half):
            rows = slice(j * scen_dev, (j + 1) * scen_dev)
            partial[0, step, j] = netted[rows, :own_sets]
            partial[1, step, j] = netted[rows, own_sets:]
        swap = pltpu.make_async_remote_copy(
            src_ref=partial.at[1 - parity, step],
            dst_ref=got_pair.at[step],
            send_sem=pair_send.at[step],
            recv_sem=pair_recv.at[step],
            device_id={"wide": partner},
            device_id_type=MESH,
        )
        swap.start()
        swaps.append(swap)

    wide_copies = []
    for step in range(2):
        swaps[step].wait()
        halved[step] = partial[parity, step] + got_pair[step]
        for k, (when, start, j) in enumerate(targets):
            if when == step:
                copy = pltpu.make_async_remote_copy(
                    src_ref=halved.at[step, j],
                    dst_ref=got_wide.at[k],
                    send_sem=wide_send.at[k],
                    recv_sem=wide_recv.at[k],
                    device_id={"wide": (start + j) * 2 + parity},
                    device_id_type=MESH,
                )
                copy.start()
                wide_copies.append(copy)
    total = halved[1, place]
    for k in range(len(targets) - 1, -1, -1):
        wide_copies[k].wait()
        total += got_wide[k]

    exposure = jnp.maximum(total, 0.0)
    hit = jnp.where(default_step[...] == STEP, exposure, 0.0)
    sums[group, 0:1] = jnp.sum(exposure, axis=0, keepdims=True)
    sums[group, 1:2] = jnp.sum(hit, axis=0, keepdims=True)
    sum_copies = [
        pltpu.make_async_remote_copy(
            src_ref=sums.at[group],
            dst_ref=sums.at[group],
            send_sem=sum_send.at[k],
            recv_sem=sum_recv.at[k],
            device_id={"narrow": peer},
            device_id_type=MESH,
        )
        for k, peer in enumerate(narrow_peers)
    ]
    for copy in sum_copies:
        copy.start()
    for copy in sum_copies:
        copy.wait()
    both = sums[0]
    for n in range(1, narrow_count):
        both += sums[n]
    sums_out[...] = both


def on_device(
    shocks,
    load_tiles,
    load_index,
    delta_tiles,
    delta_index,
    base_value,
    trade_set,
    set_slot,
    default_step,
):
    narrow_count = lax.axis_size("narrow")
    wide_count = lax.axis_size("wide")
    scen_all, width = shocks.shape
    factor_blocks = width // BLOCK
    own_blocks = factor_blocks // narrow_count
    scen_dev, own_sets = default_step.shape
    trades = trade_set.shape[0]
    couples = wide_count // 2
    lines = couples * scen_dev
    dma = pltpu.SemaphoreType.DMA
    arrays = (
        shocks,
        load_tiles,
        load_index.T,
        delta_tiles,
        delta_index.T,
        base_value.reshape(-1, BLOCK),
        trade_set.reshape(-1, BLOCK),
        set_slot.reshape(-1, BLOCK),
        default_step,
    )
    spaces = [pltpu.VMEM, pltpu.VMEM, pltpu.SMEM, pltpu.VMEM, pltpu.SMEM] + [pltpu.VMEM] * 4
    totals = pl.pallas_call(
        functools.partial(kernel, narrow_count, wide_count),
        out_shape=pltpu.VMEM((2, own_sets), F32),
        in_specs=[pl.BlockSpec(memory_space=pl.ANY)] * len(arrays),
        out_specs=pl.BlockSpec(memory_space=pltpu.VMEM),
        scratch_shapes=[space(array.shape, array.dtype) for space, array in zip(spaces, arrays)]
        + [
            pltpu.VMEM((factor_blocks, scen_all, BLOCK), BF16),
            pltpu.VMEM((narrow_count, own_blocks, scen_dev, BLOCK), BF16),
            pltpu.VMEM((factor_blocks, scen_dev, BLOCK), BF16),
            pltpu.VMEM((load_tiles.shape[0], scen_all, BLOCK), F32),
            pltpu.VMEM((2 * own_sets, trades), BF16),
            pltpu.VMEM((lines, trades), BF16),
            pltpu.VMEM((2, lines, trades), BF16),
            pltpu.VMEM((2, 2, couples // 2, scen_dev, own_sets), F32),
            pltpu.VMEM((2, couples // 2, scen_dev, own_sets), F32),
            pltpu.VMEM((2, couples // 2, scen_dev, own_sets), F32),
            pltpu.VMEM((couples - 1, scen_dev, own_sets), F32),
            pltpu.VMEM((narrow_count, 2, own_sets), F32),
            dma((len(arrays),)),
            dma((narrow_count - 1,)),
            dma((narrow_count - 1,)),
            dma((2,)),
            dma((2,)),
            dma((couples - 1,)),
            dma((couples - 1,)),
            dma((narrow_count - 1,)),
            dma((narrow_count - 1,)),
        ],
        compiler_params=pltpu.CompilerParams(collective_id=0, has_side_effects=True),
    )(*arrays)
    return totals[0] / scen_all, totals[1] * (STEPS / scen_all)


def solution(mesh):
    return jax.shard_map(
        on_device,
        mesh=mesh,
        in_specs=(
            P(),
            P("narrow", None, None),
            P("narrow", None),
            P("wide", None, None),
            P("wide", None),
            P("wide"),
            P("wide"),
            P(),
            P("narrow", "wide"),
        ),
        out_specs=(P("wide"), P("wide")),
        check_vma=False,
    )
```
